32 devices in a mesh: wide: 8 (over y, x, core), narrow: 4 (over z).
Axes of the slice: x: 2, y: 2, z: 4, core: 2. Of those that a mesh axis runs over, the one named last changes fastest.
Arguments:
- source_features: float32 [50, 16384], P(None, ('wide', 'narrow')), may hold values from -24 to 24
- target_features: float32 [50, 65536], P(None, 'narrow'), may hold values from -24 to 24
- source_mass: float32 [16384], P('wide'), may hold values from 0.05 to 20
- target_mass: float32 [65536], P('narrow'), may hold values from 0.05 to 20
- block_cols: int32 [128, 32], P('wide', 'narrow'), may hold values from 0 to 127, as said below
- block_counts: int32 [128, 4], P('wide', 'narrow'), may hold values from 1 to 8, as said below
Outputs:
- row_potential: float32 [16384], P('wide')
- col_potential: float32 [65536], P('narrow')
The draws below stay inside these ranges and needn't reach their ends.
Inputs may be any that keep to these rules, and one draw needn't show every extreme that they name: `block_cols`: each list of 8 entries holds distinct column tile ids of its group; every column tile of every group is the first entry of some row tile's list. `block_counts`: on the 16 row tiles of one index of wide and one column group the counts sum to at most 96, and to exactly 96 on some such device.
All inputs are finite; a program needn't handle non-finite values.
Results may differ from the reference program's by a relative error of at most 0.0003.
Values sent between devices are 32-bit elements; how exact they have to be, the bound alone decides.
A program may use at most 64 MiB of HBM per device.

```python
import math
import jax
import jax.numpy as jnp
from jax import lax

F = 50
TILE = 128
RT_DEV = 16
CT_DEV = 128
K_MAX = 8
ITERS = 2
ROW_GROUPS = 8
COL_GROUPS = 4
ROW_TILES = 128
ROWS = 16384
COLS = 65536
LIVE_MAX = 96


def draw_source_features(key, part):
    values = jnp.clip(jax.random.normal(key, (F, ROWS), jnp.float32), -6.0, 6.0)
    return values


def draw_target_features(key, part):
    values = jnp.clip(jax.random.normal(jax.random.fold_in(key, 3), (F, COLS), jnp.float32), -6.0, 6.0)
    return values


def draw_block_counts(key, part):
    key_total, key_heavy, key_units, key_tiles = jax.random.split(jax.random.fold_in(key, 21), 4)
    device_count = ROW_GROUPS * COL_GROUPS
    upper = max(RT_DEV, RT_DEV * K_MAX // 4)
    totals = jax.random.randint(key_total, (device_count,), RT_DEV, upper + 1)
    heaviest = jax.random.randint(key_heavy, (), 0, device_count)
    unit_count = RT_DEV * (K_MAX - 1)
    subkeys = jax.random.split(key_units, device_count)
    shuffled = jax.vmap(lambda subkey: jax.random.permutation(subkey, unit_count))(subkeys)
    needed = totals - RT_DEV
    chosen = jnp.arange(unit_count, dtype=jnp.int32)[None, :] < needed[:, None]
    owner = shuffled // (K_MAX - 1)
    belongs = (owner[:, :, None] == jnp.arange(RT_DEV, dtype=jnp.int32)[None, None, :]) & chosen[:, :, None]
    extras = jnp.sum(belongs.astype(jnp.int32), axis=1)
    tile_order = jax.random.permutation(key_tiles, RT_DEV)
    sequential = jnp.clip(LIVE_MAX - RT_DEV - tile_order * (K_MAX - 1), 0, K_MAX - 1)
    is_heavy = (jnp.arange(device_count, dtype=jnp.int32) == heaviest)[:, None]
    extras = jnp.where(is_heavy, sequential[None, :], extras)
    counts = 1 + extras
    counts = counts.reshape(ROW_GROUPS, COL_GROUPS, RT_DEV).transpose(0, 2, 1).reshape(ROW_TILES, COL_GROUPS)
    return counts.astype(jnp.int32)


def draw_block_cols(key, part):
    key_cover, key_others = jax.random.split(jax.random.fold_in(key, 33), 2)
    cover_keys = jax.random.split(key_cover, COL_GROUPS)
    coverage = jax.vmap(lambda subkey: jax.random.permutation(subkey, CT_DEV))(cover_keys)
    leading = coverage[:, jnp.arange(ROW_TILES, dtype=jnp.int32) % CT_DEV].T
    other_keys = jax.random.split(key_others, ROW_TILES * COL_GROUPS)
    others = jax.vmap(lambda subkey: jax.random.permutation(subkey, CT_DEV - 1)[:K_MAX - 1])(other_keys)
    others = others.reshape(ROW_TILES, COL_GROUPS, K_MAX - 1)
    following = (leading[:, :, None] + 1 + others) % CT_DEV
    lists = jnp.concatenate([leading[:, :, None], following], axis=2).reshape(ROW_TILES, COL_GROUPS * K_MAX)
    return lists.astype(jnp.int32)


def shard_levels(key, extent, cuts, low, largest):
    def one(position, blocks):
        heights = jax.random.uniform(jax.random.fold_in(jax.random.fold_in(key, 6), position), (blocks,), jnp.float32, low / len(cuts), largest / len(cuts))
        return jnp.repeat(jnp.exp(heights), extent[position] // blocks).reshape((-1,) + (1,) * (len(extent) - position - 1))

    factor_of = one(*cuts[0])
    for cut in cuts[1:]:
        factor_of = factor_of * one(*cut)
    return factor_of


def setup_inputs(seed: int = 0) -> dict:
    arg_keys = jax.random.split(jax.random.key(seed), 7)
    return {
        "source_features": draw_source_features(jax.random.fold_in(arg_keys[6], 71), 0),
        "target_features": draw_target_features(jax.random.fold_in(arg_keys[6], 71), 0),
        "source_mass": jnp.clip(jnp.exp(math.log(20.0) - 5.9914645 * jax.random.uniform(arg_keys[2], (ROWS,), jnp.float32) ** shard_levels(arg_keys[2], (ROWS,), ((0, 8),), -0.2, 0.2)), 0.05, 20.0),
        "target_mass": jnp.clip(jnp.exp(math.log(20.0) - 5.9914645 * jax.random.uniform(arg_keys[3], (COLS,), jnp.float32) ** shard_levels(arg_keys[3], (COLS,), ((0, 4),), -0.2, 0.2)), 0.05, 20.0),
        "block_cols": draw_block_cols(jax.random.fold_in(arg_keys[6], 71), 0),
        "block_counts": draw_block_counts(jax.random.fold_in(arg_keys[6], 71), 0),
    }


epsilon = 0.05
very_low = -1e30


def reference(source_features, target_features, source_mass, target_mass, block_cols, block_counts):
    col_total = COL_GROUPS * CT_DEV
    source_norm = jnp.sum(source_features * source_features, axis=0)
    target_norm = jnp.sum(target_features * target_features, axis=0)
    source_tiles = source_features.reshape(F, ROW_TILES, TILE)
    target_tiles = target_features.reshape(F, col_total, TILE)
    source_norm_tiles = source_norm.reshape(ROW_TILES, TILE)
    target_norm_tiles = target_norm.reshape(col_total, TILE)
    group_base = (jnp.arange(COL_GROUPS, dtype=jnp.int32) * CT_DEV)[None, :, None]
    global_cols = (block_cols.reshape(ROW_TILES, COL_GROUPS, K_MAX).astype(jnp.int32) + group_base).reshape(ROW_TILES, COL_GROUPS * K_MAX).astype(jnp.int32)
    is_live = (jnp.arange(K_MAX, dtype=jnp.int32)[None, None, :] < block_counts[:, :, None]).reshape(ROW_TILES, COL_GROUPS * K_MAX)

    def cost_tiles(row_tile):
        columns = global_cols[row_tile]
        source_part = source_tiles[:, row_tile, :]
        target_part = jnp.take(target_tiles, columns, axis=1)
        inner = jnp.einsum('fa,fsb->sab', source_part, target_part, precision=lax.Precision.HIGHEST)
        cost_tile = (source_norm_tiles[row_tile][None, :, None] + target_norm_tiles[columns][:, None, :] - 2.0 * inner) / F
        return cost_tile, columns, is_live[row_tile]

    def row_update(col_values):
        col_tiles = col_values.reshape(col_total, TILE)

        def one_tile(row_tile):
            cost_tile, columns, alive = cost_tiles(row_tile)
            scores = (col_tiles[columns][:, None, :] - cost_tile) / epsilon
            scores = jnp.where(alive[:, None, None], scores, very_low)
            highest = jnp.max(scores, axis=(0, 2))
            summed = jnp.sum(jnp.where(alive[:, None, None], jnp.exp(scores - highest[None, :, None]), 0.0), axis=(0, 2))
            return highest + jnp.log(summed)

        totals = lax.map(one_tile, jnp.arange(ROW_TILES, dtype=jnp.int32)).reshape(-1)
        return epsilon * jnp.log(source_mass) - epsilon * totals

    def col_update(row_values):
        row_tiles = row_values.reshape(ROW_TILES, TILE)

        def one_tile(running, row_tile):
            highest, summed = running
            cost_tile, columns, alive = cost_tiles(row_tile)
            scores = (row_tiles[row_tile][None, :, None] - cost_tile) / epsilon
            peaks = jnp.max(scores, axis=1)
            masses = jnp.sum(jnp.exp(scores - peaks[:, None, :]), axis=1)
            old_high = highest[columns]
            old_sum = summed[columns]
            new_high = jnp.maximum(old_high, peaks)
            new_sum = old_sum * jnp.exp(old_high - new_high) + masses * jnp.exp(peaks - new_high)
            target_index = jnp.where(alive, columns, col_total).astype(jnp.int32)
            highest = highest.at[target_index].set(new_high, mode='drop')
            summed = summed.at[target_index].set(new_sum, mode='drop')
            return (highest, summed), None

        initial = (jnp.full((col_total, TILE), very_low, jnp.float32), jnp.zeros((col_total, TILE), jnp.float32))
        (highest, summed), _ = lax.scan(one_tile, initial, jnp.arange(ROW_TILES, dtype=jnp.int32))
        return epsilon * jnp.log(target_mass) - epsilon * (highest.reshape(-1) + jnp.log(summed.reshape(-1)))

    col_values = jnp.zeros((col_total * TILE,), jnp.float32)
    row_values = jnp.zeros((ROW_TILES * TILE,), jnp.float32)
    for iteration in range(ITERS):
        row_values = row_update(col_values)
        col_values = col_update(row_values)
    return row_values, col_values
```

```python
import functools

import jax
import jax.numpy as jnp
from jax import lax
from jax.experimental import pallas as pl
from jax.experimental.pallas import tpu as pltpu
from jax.sharding import PartitionSpec as P

F = 50
TILE = 128
K_MAX = 8
ITERS = 2
PAD = 64
CHUNKS = 4
SLAB = 8
UNROLL = 4
COL_UNROLL = 2
PARTS = (1, 2)

epsilon = 0.05
very_low = -1e30
log2_e = 1.4426950408889634
product_scale = 2.0 * log2_e / (F * epsilon)
norm_scale = log2_e / (F * epsilon)
potential_scale = epsilon / log2_e


def split_three(x):
    first = x.astype(jnp.bfloat16)
    rest = x - first.astype(jnp.float32)
    second = rest.astype(jnp.bfloat16)
    third = (rest - second.astype(jnp.float32)).astype(jnp.bfloat16)
    return first, second, third


def log2(x):
    return jnp.log(x) * log2_e


def paired(me, d, size):
    other, bit = 0, 1
    while bit < size:
        other = other + lax.rem(lax.div(me, bit) + d // bit % 2, 2) * bit
        bit *= 2
    return other


def tree(combine, parts):
    parts = list(parts)
    while len(parts) > 1:
        pairs = [combine(a, b) for a, b in zip(parts[0::2], parts[1::2])]
        parts = pairs + parts[len(parts) // 2 * 2 :]
    return parts[0]


def padded(x):
    return jnp.concatenate([x, jnp.zeros((PAD - F, TILE), jnp.float32)], axis=0)


def packing(shard_tiles):
    rest = F % SLAB
    extra = -(-shard_tiles * rest // SLAB) * SLAB
    full = F - rest
    pieces = 2 if shard_tiles % 2 == 0 else 1
    per_piece = shard_tiles // pieces
    ends = [extra + (p + 1) * per_piece * full for p in range(pieces)]
    return rest, extra, full, per_piece, list(zip([0] + ends[:-1], ends))


def kernel(
    wide_size,
    narrow_size,
    cols_ref,
    counts_ref,
    source_hbm,
    target_hbm,
    row_mass_hbm,
    col_mass_hbm,
    row_out_ref,
    col_out_ref,
    source_ref,
    gathered,
    target_ref,
    row_mass_ref,
    col_mass_ref,
    right,
    scores,
    one_hot,
    one_hot_rows,
    one_hot_cols,
    marked,
    source_norm,
    target_norm,
    col_values,
    col_pieces,
    row_values,
    row_factor,
    row_send,
    row_recv,
    tops,
    slot_peak,
    slot_mass,
    col_send,
    col_recv,
    load_sem,
    gather_send_sem,
    forward_send_sem,
    gather_recv_sem,
    row_send_sem,
    row_recv_sem,
    scatter_send_sem,
    scatter_recv_sem,
    spread_send_sem,
    spread_recv_sem,
):
    wide = lax.axis_index("wide")
    narrow = lax.axis_index("narrow")
    row_count = row_mass_ref.shape[0]
    col_count = col_mass_ref.shape[0]
    shard_tiles = row_count // narrow_size
    piece = col_count // wide_size
    chunk_tiles = col_count // CHUNKS
    chunk_cols = chunk_tiles * TILE
    slabs = TILE // SLAB
    rest, extra, full, per_piece, spans = packing(shard_tiles)
    reach = max(1, narrow_size // 2)

    def wide_peer(d):
        return paired(wide, d, wide_size)

    def narrow_peer(d):
        return paired(narrow, d, narrow_size)

    def at_wide(w):
        return {"wide": w, "narrow": narrow}

    def at_narrow(z):
        return {"wide": wide, "narrow": z}

    def remote(src, dst, send, recv, where):
        return pltpu.make_async_remote_copy(
            src_ref=src,
            dst_ref=dst,
            send_sem=send,
            recv_sem=recv,
            device_id=where,
            device_id_type=pl.DeviceIdType.MESH,
        )

    barrier = pltpu.get_barrier_semaphore()
    for d in range(1, narrow_size):
        pl.semaphore_signal(
            barrier, inc=1, device_id=at_narrow(narrow_peer(d)), device_id_type=pl.DeviceIdType.MESH
        )
    for d in range(1, wide_size):
        pl.semaphore_signal(
            barrier, inc=1, device_id=at_wide(wide_peer(d)), device_id_type=pl.DeviceIdType.MESH
        )
    loads = [pltpu.make_async_copy(source_hbm, source_ref, load_sem.at[CHUNKS])]
    for q in range(CHUNKS):
        part = pl.ds(q * chunk_cols, chunk_cols)
        loads.append(
            pltpu.make_async_copy(target_hbm.at[:, part], target_ref.at[:, part], load_sem.at[q])
        )
    loads.append(pltpu.make_async_copy(row_mass_hbm, row_mass_ref, load_sem.at[CHUNKS + 1]))
    loads.append(pltpu.make_async_copy(col_mass_hbm, col_mass_ref, load_sem.at[CHUNKS + 2]))
    for load in loads:
        load.start()

    loads[0].wait()
    tiles = [slice(t * TILE, (t + 1) * TILE) for t in range(shard_tiles)]
    left = [source_ref[full:F, tile] for tile in tiles]
    fill = extra - rest * shard_tiles
    if fill:
        left.append(jnp.zeros((fill, TILE), jnp.float32))
    gathered[narrow, 0:extra, :] = jnp.concatenate(left, axis=0)
    for t, tile in enumerate(tiles):
        gathered[narrow, extra + t * full : extra + (t + 1) * full, :] = source_ref[0:full, tile]
    pl.semaphore_wait(barrier, narrow_size + wide_size - 2)

    def block_copy(block, p, send, step):
        part = gathered.at[block, spans[p][0] : spans[p][1]]
        return remote(part, part, send, gather_recv_sem.at[block, p], at_narrow(narrow + step))

    own_steps = [
        sign * distance
        for distance in [reach] + list(range(1, reach))
        for sign in (1, -1)
    ]

    def inside(step):
        return (narrow + step >= 0) & (narrow + step < narrow_size)

    def own_copies(act):
        for i, step in enumerate(own_steps):

            @pl.when(inside(step))
            def _():
                for p in range(len(spans)):
                    act(block_copy(narrow, p, gather_send_sem.at[i, p], step))

    def forward_copies(act, p):
        block = narrow_peer(reach)
        for distance in range(1, narrow_size - reach):
            for sign in (1, -1):
                below = narrow > block if sign > 0 else narrow < block

                @pl.when(below & inside(sign * distance))
                def _():
                    act(block_copy(block, p, forward_send_sem.at[distance - 1, p], sign * distance))

    own_copies(lambda copy: copy.start())

    def prepare_target(g, carry):
        for u in range(UNROLL):
            c = g * UNROLL + u
            x = padded(target_ref[:, pl.ds(pl.multiple_of(c * TILE, TILE), TILE)])
            first, second, third = split_three(x)
            right[c, 0:PAD, :] = first
            right[c, PAD : 2 * PAD, :] = second
            right[c, 2 * PAD : 3 * PAD, :] = third
            target_norm[pl.ds(c, 1), :] = jnp.sum(x * x, axis=0, keepdims=True) * norm_scale
        return carry

    for q in range(CHUNKS):
        loads[q + 1].wait()
        lax.fori_loop(
            q * chunk_tiles // UNROLL, (q + 1) * chunk_tiles // UNROLL, prepare_target, 0
        )
    loads[CHUNKS + 1].wait()
    loads[CHUNKS + 2].wait()

    lane = lax.broadcasted_iota(jnp.int32, (1, TILE), 1)

    def product_tile(r, x):
        source_norm[pl.ds(r, 1), :] = jnp.sum(x * x, axis=0, keepdims=True) * norm_scale
        first, second, third = split_three(x * product_scale)
        leading = jnp.transpose(jnp.concatenate([first, second], axis=0))
        trailing = jnp.transpose(jnp.concatenate([first, third], axis=0))
        a = jnp.concatenate([leading, leading, trailing], axis=1)
        marks = []
        for k in range(0, K_MAX, 2):
            pair = []
            for j in (k, k + 1):
                c = cols_ref[j, r]
                first_part = right[c, 0:PAD, :]
                second_part = right[c, PAD : 2 * PAD, :]
                third_part = right[c, 2 * PAD : 3 * PAD, :]
                pair.append(
                    jnp.concatenate(
                        [first_part, first_part, second_part, second_part, third_part, first_part],
                        axis=0,
                    )
                )
                alive = j < counts_ref[0, r]
                marks.append((lane == jnp.where(alive, c, -1)).astype(jnp.float32))
            product = jnp.dot(
                a, jnp.concatenate(pair, axis=1), preferred_element_type=jnp.float32
            )
            for j in (k, k + 1):
                scores[r * K_MAX + j] = product[:, (j - k) * TILE : (j - k + 1) * TILE]
        marks = jnp.concatenate(marks, axis=0)
        one_hot[pl.ds(pl.multiple_of(r * K_MAX, K_MAX), K_MAX), :] = marks
        unmarked = 1.0 - jnp.sum(marks, axis=0, keepdims=True)
        marked[r] = jnp.concatenate(
            [marks, marks, unmarked, jnp.zeros((2 * K_MAX - 1, TILE), jnp.float32)], axis=0
        ).astype(jnp.bfloat16)

    def first_row_tile(r):
        values = []
        for k in range(K_MAX):
            value = jnp.where(
                k < counts_ref[0, r], -target_norm[pl.ds(cols_ref[k, r], 1), :], very_low
            )
            values.append(jnp.broadcast_to(value, (SLAB, TILE)))
        peaks, masses = [], []
        for h in range(slabs):
            rows = slice(h * SLAB, (h + 1) * SLAB)
            s = [scores[r * K_MAX + k, rows, :] + values[k] for k in range(K_MAX)]
            top = tree(jnp.maximum, s)
            masses.append(tree(jnp.add, [jnp.exp2(x - top) for x in s]))
            peaks.append(top)
        peaks = jnp.transpose(jnp.concatenate(peaks, axis=0))
        masses = jnp.transpose(jnp.concatenate(masses, axis=0))
        peak = jnp.max(peaks, axis=0, keepdims=True)
        mass = jnp.sum(masses * jnp.exp2(peaks - peak), axis=0, keepdims=True)
        row_send[0, pl.ds(r, 1), :] = peak + log2(mass)

    previous = None
    order = [0, reach] + [d for d in range(1, narrow_size) if d != reach]
    for d in order:
        z = narrow if d == 0 else narrow_peer(d)
        for p in range(len(spans)):
            if d > 0:
                block_copy(z, p, gather_send_sem.at[0, p], z - narrow).wait_recv()
            if d == reach:
                forward_copies(lambda copy: copy.start(), p)
            for t in range(p * per_piece, (p + 1) * per_piece):
                x = padded(
                    jnp.concatenate(
                        [
                            gathered[z, extra + t * full : extra + (t + 1) * full, :],
                            gathered[z, t * rest : (t + 1) * rest, :],
                        ],
                        axis=0,
                    )
                )
                r = z * shard_tiles + t
                if previous is not None:
                    first_row_tile(previous)
                product_tile(r, x)
                previous = r
    first_row_tile(previous)

    def exchange(axis_size, peer, where, src_of, buffer, me, send_sem, recv_sem):
        for d in range(1, axis_size):
            to = peer(d)
            remote(src_of(to), buffer.at[me], send_sem, recv_sem, where(to)).start()

        def finish():
            everything = buffer.at[0 : axis_size - 1]
            whole = remote(everything, everything, send_sem, recv_sem, where(peer(1)))
            whole.wait_recv()
            whole.wait_send()

        return finish

    def row_share(step, part):
        count = row_count // PARTS[step]
        rows = slice(part * count, (part + 1) * count)
        row_recv[step, narrow, rows, :] = row_send[step, rows, :]
        everything = row_recv.at[step, :, rows]
        return exchange(
            narrow_size,
            narrow_peer,
            at_narrow,
            lambda to: row_send.at[step, rows],
            everything,
            narrow,
            row_send_sem.at[step, part],
            row_recv_sem.at[step, part],
        )

    def row_combine(step, part):
        count = row_count // PARTS[step]
        rows = slice(part * count, (part + 1) * count)
        parts = [row_recv[step, z, rows, :] for z in range(narrow_size)]
        mass = row_mass_ref[rows, :]
        if step == 0:
            top = functools.reduce(jnp.maximum, parts)
            total = sum(jnp.exp2(p - top) for p in parts)
            row_values[rows, :] = log2(mass) - (top + log2(total))
        else:
            total = sum(parts)
            row_factor[rows, :] = mass / total
            row_out_ref[rows, :] = potential_scale * (
                row_values[rows, :] + log2(mass) - log2(total) + source_norm[rows, :]
            )

    def spread_rows(ref, r):
        return jnp.transpose(jnp.broadcast_to(ref[pl.ds(r, 1), :], (TILE, TILE)))

    def first_col_tile(r):
        values = spread_rows(row_values, r)
        peaks, masses = [], []
        for k in range(K_MAX):
            slot = r * K_MAX + k
            s = [
                scores[slot, h * SLAB : (h + 1) * SLAB, :] + values[h * SLAB : (h + 1) * SLAB]
                for h in range(slabs)
            ]
            top = tree(jnp.maximum, s)
            terms = [jnp.exp2(x - top) for x in s]
            for h in range(slabs):
                scores[slot, h * SLAB : (h + 1) * SLAB, :] = terms[h]
            total = tree(jnp.add, terms)
            peak = jnp.max(top, axis=0, keepdims=True)
            masses.append(jnp.sum(total * jnp.exp2(top - peak), axis=0, keepdims=True))
            alive = k < counts_ref[0, r]
            tops[slot] = jnp.where(alive, top, very_low)
            peaks.append(jnp.where(alive, peak, very_low))
        place = pl.ds(pl.multiple_of(r * K_MAX, K_MAX), K_MAX)
        slot_peak[place, :] = jnp.concatenate(peaks, axis=0)
        slot_mass[place, :] = jnp.concatenate(masses, axis=0)

    def second_row_tile(r):
        total = [None] * slabs
        for k in range(K_MAX):
            slot = r * K_MAX + k
            factor = jnp.exp2(
                tops[slot]
                + jnp.broadcast_to(col_values[pl.ds(cols_ref[k, r], 1), :], (SLAB, TILE))
            )
            tops[slot] = factor
            for h in range(slabs):
                term = scores[slot, h * SLAB : (h + 1) * SLAB, :] * factor
                total[h] = term if k == 0 else total[h] + term
        turned = jnp.transpose(jnp.concatenate(total, axis=0))
        row_send[1, pl.ds(r, 1), :] = jnp.sum(turned, axis=0, keepdims=True)

    def second_col_tile(r):
        values = spread_rows(row_factor, r)
        masses = []
        for k in range(K_MAX):
            slot = r * K_MAX + k
            total = tree(
                jnp.add,
                [
                    scores[slot, h * SLAB : (h + 1) * SLAB, :] * values[h * SLAB : (h + 1) * SLAB]
                    for h in range(slabs)
                ],
            )
            masses.append(jnp.sum(total * tops[slot], axis=0, keepdims=True))
        place = pl.ds(pl.multiple_of(r * K_MAX, K_MAX), K_MAX)
        slot_mass[place, :] = jnp.concatenate(masses, axis=0)

    def over_tiles(step, part, one_tile):
        count = row_count // PARTS[step]

        def some(g, carry):
            for u in range(COL_UNROLL):
                one_tile(g * COL_UNROLL + u)
            return carry

        lax.fori_loop(part * count // COL_UNROLL, (part + 1) * count // COL_UNROLL, some, 0)

    def split_two(x, axis):
        coarse = x.astype(jnp.bfloat16)
        fine = (x - coarse.astype(jnp.float32)).astype(jnp.bfloat16)
        return jnp.concatenate([coarse, fine], axis=axis)

    def column_sums(x):
        return jnp.dot(
            one_hot_cols[...], split_two(x, 0), preferred_element_type=jnp.float32
        )

    def column_lse():
        high = None
        for r in range(row_count):
            peaks = slot_peak[r * K_MAX : (r + 1) * K_MAX, :]
            coarse = peaks.astype(jnp.bfloat16).astype(jnp.float32)
            stack = jnp.concatenate(
                [
                    coarse,
                    peaks - coarse,
                    jnp.full((1, TILE), very_low, jnp.float32),
                    jnp.zeros((2 * K_MAX - 1, TILE), jnp.float32),
                ],
                axis=0,
            ).astype(jnp.bfloat16)
            spread = lax.dot_general(
                marked[r],
                stack,
                (((0,), (0,)), ((), ())),
                preferred_element_type=jnp.float32,
            )
            high = spread if high is None else jnp.maximum(high, spread)
        found = jnp.dot(
            one_hot_rows[...], split_two(high, 1), preferred_element_type=jnp.float32
        )
        found = found[:, 0:TILE] + found[:, TILE : 2 * TILE]
        summed = column_sums(slot_mass[...] * jnp.exp2(jnp.minimum(slot_peak[...] - found, 1e2)))
        return jnp.where(summed > 0.0, high + log2(jnp.maximum(summed, 1e-30)), very_low)

    def columns_share(step, sums):
        for w in range(wide_size):
            col_send[step, w] = sums[w * piece : (w + 1) * piece]
        finish = exchange(
            wide_size,
            wide_peer,
            at_wide,
            lambda to: col_send.at[step, to],
            col_recv.at[step],
            wide,
            scatter_send_sem.at[step],
            scatter_recv_sem.at[step],
        )
        col_recv[step, wide] = col_send[step, wide]
        finish()
        parts = [col_recv[step, w] for w in range(wide_size)]
        rows = pl.ds(pl.multiple_of(wide * piece, piece), piece)
        mass = col_mass_ref[rows, :]
        if step == 0:
            top = tree(jnp.maximum, parts)
            total = tree(jnp.add, [jnp.exp2(p - top) for p in parts])
            col_pieces[step, wide] = log2(mass) - (top + log2(total))
        else:
            total = tree(jnp.add, parts)
            col_pieces[step, wide] = potential_scale * (
                col_values[rows, :] + log2(mass) - log2(total) + target_norm[rows, :]
            )
        finish = exchange(
            wide_size,
            wide_peer,
            at_wide,
            lambda to: col_pieces.at[step, wide],
            col_pieces.at[step],
            wide,
            spread_send_sem.at[step],
            spread_recv_sem.at[step],
        )
        finish()
        where = col_values if step == 0 else col_out_ref
        for w in range(wide_size):
            where[w * piece : (w + 1) * piece, :] = col_pieces[step, w]

    finish = row_share(0, 0)
    one_hot_rows[...] = one_hot[...].astype(jnp.bfloat16)
    turned = jnp.transpose(one_hot[...]).astype(jnp.bfloat16)
    one_hot_cols[...] = jnp.concatenate([turned, turned], axis=1)
    own_copies(lambda copy: copy.wait_send())
    for p in range(len(spans)):
        forward_copies(lambda copy: copy.wait_send(), p)
    finish()
    row_combine(0, 0)
    over_tiles(0, 0, first_col_tile)
    columns_share(0, column_lse())

    finishes = []
    for part in range(PARTS[1]):
        over_tiles(1, part, second_row_tile)
        finishes.append(row_share(1, part))
    for part in range(PARTS[1]):
        finishes[part]()
        row_combine(1, part)
        over_tiles(1, part, second_col_tile)
    columns_share(1, column_sums(slot_mass[...]))


def local(
    wide_size,
    narrow_size,
    source_features,
    target_features,
    source_mass,
    target_mass,
    block_cols,
    block_counts,
):
    row_count = source_mass.shape[0] // TILE
    col_count = target_mass.shape[0] // TILE
    slots = row_count * K_MAX
    piece = col_count // wide_size
    spans = packing(row_count // narrow_size)[-1]
    reach = max(1, narrow_size // 2)
    vmem = pl.BlockSpec(memory_space=pltpu.VMEM)
    smem = pl.BlockSpec(memory_space=pltpu.SMEM)
    hbm = pl.BlockSpec(memory_space=pltpu.HBM)
    f32 = jnp.float32
    bf16 = jnp.bfloat16
    dma = pltpu.SemaphoreType.DMA
    rows, cols = pl.pallas_call(
        functools.partial(kernel, wide_size, narrow_size),
        out_shape=(
            jax.ShapeDtypeStruct((row_count, TILE), f32),
            jax.ShapeDtypeStruct((col_count, TILE), f32),
        ),
        in_specs=[smem, smem, hbm, hbm, hbm, hbm],
        out_specs=(vmem, vmem),
        scratch_shapes=[
            pltpu.VMEM(source_features.shape, f32),
            pltpu.VMEM((narrow_size, spans[-1][1], TILE), f32),
            pltpu.VMEM(target_features.shape, f32),
            pltpu.VMEM((row_count, TILE), f32),
            pltpu.VMEM((col_count, TILE), f32),
            pltpu.VMEM((col_count, 3 * PAD, TILE), bf16),
            pltpu.VMEM((slots, TILE, TILE), f32),
            pltpu.VMEM((slots, col_count), f32),
            pltpu.VMEM((slots, col_count), bf16),
            pltpu.VMEM((col_count, 2 * slots), bf16),
            pltpu.VMEM((row_count, 4 * K_MAX, col_count), bf16),
            pltpu.VMEM((row_count, TILE), f32),
            pltpu.VMEM((col_count, TILE), f32),
            pltpu.VMEM((col_count, TILE), f32),
            pltpu.VMEM((ITERS, wide_size, piece, TILE), f32),
            pltpu.VMEM((row_count, TILE), f32),
            pltpu.VMEM((row_count, TILE), f32),
            pltpu.VMEM((ITERS, row_count, TILE), f32),
            pltpu.VMEM((ITERS, narrow_size, row_count, TILE), f32),
            pltpu.VMEM((slots, SLAB, TILE), f32),
            pltpu.VMEM((slots, TILE), f32),
            pltpu.VMEM((slots, TILE), f32),
            pltpu.VMEM((ITERS, wide_size, piece, TILE), f32),
            pltpu.VMEM((ITERS, wide_size, piece, TILE), f32),
            dma((CHUNKS + 3,)),
            dma((2 * reach, len(spans))),
            dma((max(1, narrow_size - 1 - reach), len(spans))),
            dma((narrow_size, len(spans))),
            dma((ITERS, max(PARTS))),
            dma((ITERS, max(PARTS))),
            dma((ITERS,)),
            dma((ITERS,)),
            dma((ITERS,)),
            dma((ITERS,)),
        ],
        compiler_params=pltpu.CompilerParams(
            collective_id=0, has_side_effects=True, vmem_limit_bytes=67043328
        ),
    )(
        block_cols.T,
        block_counts.T,
        source_features,
        target_features,
        source_mass.reshape(row_count, TILE),
        target_mass.reshape(col_count, TILE),
    )
    return rows.reshape(-1), cols.reshape(-1)


def solution(mesh):
    in_specs = (
        P(None, ("wide", "narrow")),
        P(None, "narrow"),
        P("wide"),
        P("narrow"),
        P("wide", "narrow"),
        P("wide", "narrow"),
    )
    out_specs = (P("wide"), P("narrow"))
    return jax.shard_map(
        functools.partial(local, mesh.shape["wide"], mesh.shape["narrow"]),
        mesh=mesh,
        in_specs=in_specs,
        out_specs=out_specs,
        check_vma=False,
    )
```

```python
import functools

import jax
import jax.numpy as jnp
from jax import lax
from jax.experimental import pallas as pl
from jax.experimental.pallas import tpu as pltpu
from jax.sharding import PartitionSpec as P

F = 50
TILE = 128
K_MAX = 8
ITERS = 2
PAD = 64
CHUNKS = 4
SLAB = 8
UNROLL = 4
COL_UNROLL = 2
PARTS = 2

epsilon = 0.05
very_low = -1e30
log2_e = 1.4426950408889634
product_scale = 2.0 * log2_e / (F * epsilon)
norm_scale = log2_e / (F * epsilon)
potential_scale = epsilon / log2_e


def split_three(x):
    first = x.astype(jnp.bfloat16)
    rest = x - first.astype(jnp.float32)
    second = rest.astype(jnp.bfloat16)
    third = (rest - second.astype(jnp.float32)).astype(jnp.bfloat16)
    return first, second, third


def log2(x):
    return jnp.log(x) * log2_e


def paired(me, d, size):
    other, bit = 0, 1
    while bit < size:
        other = other + lax.rem(lax.div(me, bit) + d // bit % 2, 2) * bit
        bit *= 2
    return other


def tree(combine, parts):
    parts = list(parts)
    while len(parts) > 1:
        pairs = [combine(a, b) for a, b in zip(parts[0::2], parts[1::2])]
        parts = pairs + parts[len(parts) // 2 * 2 :]
    return parts[0]


def padded(x):
    return jnp.concatenate([x, jnp.zeros((PAD - F, TILE), jnp.float32)], axis=0)


def packing(shard_tiles):
    rest = F % SLAB
    extra = -(-shard_tiles * rest // SLAB) * SLAB
    full = F - rest
    pieces = 2 if shard_tiles % 2 == 0 else 1
    per_piece = shard_tiles // pieces
    ends = [extra + (p + 1) * per_piece * full for p in range(pieces)]
    return rest, extra, full, per_piece, list(zip([0] + ends[:-1], ends))


def kernel(
    wide_size,
    narrow_size,
    cols_hbm,
    counts_hbm,
    source_hbm,
    target_hbm,
    row_mass_hbm,
    col_mass_hbm,
    row_out_ref,
    col_out_ref,
    cols_ref,
    counts_ref,
    source_ref,
    gathered,
    target_ref,
    row_mass_ref,
    col_mass_ref,
    right,
    scores,
    one_hot,
    one_hot_rows,
    one_hot_cols,
    marked,
    source_norm,
    target_norm,
    col_values,
    col_pieces,
    row_values,
    row_factor,
    row_send,
    row_recv,
    tops,
    slot_peak,
    slot_mass,
    col_send,
    col_recv,
    load_sem,
    gather_send_sem,
    forward_send_sem,
    gather_recv_sem,
    row_send_sem,
    row_recv_sem,
    scatter_send_sem,
    scatter_recv_sem,
    spread_send_sem,
    spread_recv_sem,
):
    wide = lax.axis_index("wide")
    narrow = lax.axis_index("narrow")
    row_count = row_mass_ref.shape[0]
    col_count = col_mass_ref.shape[0]
    shard_tiles = row_count // narrow_size
    piece = col_count // wide_size
    chunk_tiles = col_count // CHUNKS
    chunk_cols = chunk_tiles * TILE
    slabs = TILE // SLAB
    rest, extra, full, per_piece, spans = packing(shard_tiles)
    reach = max(1, narrow_size // 2)

    def wide_peer(d):
        return paired(wide, d, wide_size)

    def narrow_peer(d):
        return paired(narrow, d, narrow_size)

    def at_wide(w):
        return {"wide": w, "narrow": narrow}

    def at_narrow(z):
        return {"wide": wide, "narrow": z}

    def remote(src, dst, send, recv, where):
        return pltpu.make_async_remote_copy(
            src_ref=src,
            dst_ref=dst,
            send_sem=send,
            recv_sem=recv,
            device_id=where,
            device_id_type=pl.DeviceIdType.MESH,
        )

    barrier = pltpu.get_barrier_semaphore()
    for d in range(1, narrow_size):
        pl.semaphore_signal(
            barrier, inc=1, device_id=at_narrow(narrow_peer(d)), device_id_type=pl.DeviceIdType.MESH
        )
    for d in range(1, wide_size):
        pl.semaphore_signal(
            barrier, inc=1, device_id=at_wide(wide_peer(d)), device_id_type=pl.DeviceIdType.MESH
        )
    loads = [pltpu.make_async_copy(source_hbm, source_ref, load_sem.at[CHUNKS])]
    for q in range(CHUNKS):
        part = pl.ds(q * chunk_cols, chunk_cols)
        loads.append(
            pltpu.make_async_copy(target_hbm.at[:, part], target_ref.at[:, part], load_sem.at[q])
        )
    loads.append(pltpu.make_async_copy(row_mass_hbm, row_mass_ref, load_sem.at[CHUNKS + 1]))
    loads.append(pltpu.make_async_copy(col_mass_hbm, col_mass_ref, load_sem.at[CHUNKS + 2]))
    loads.append(pltpu.make_async_copy(cols_hbm, cols_ref, load_sem.at[CHUNKS + 3]))
    loads.append(pltpu.make_async_copy(counts_hbm, counts_ref, load_sem.at[CHUNKS + 4]))
    for load in loads:
        load.start()

    loads[0].wait()
    tiles = [slice(t * TILE, (t + 1) * TILE) for t in range(shard_tiles)]
    left = [source_ref[full:F, tile] for tile in tiles]
    fill = extra - rest * shard_tiles
    if fill:
        left.append(jnp.zeros((fill, TILE), jnp.float32))
    gathered[narrow, 0:extra, :] = jnp.concatenate(left, axis=0)
    for t, tile in enumerate(tiles):
        gathered[narrow, extra + t * full : extra + (t + 1) * full, :] = source_ref[0:full, tile]
    pl.semaphore_wait(barrier, narrow_size + wide_size - 2)

    def block_copy(block, p, send, step):
        part = gathered.at[block, spans[p][0] : spans[p][1]]
        return remote(part, part, send, gather_recv_sem.at[block, p], at_narrow(narrow + step))

    own_steps = [
        sign * distance
        for distance in [reach] + list(range(1, reach))
        for sign in (1, -1)
    ]

    def inside(step):
        return (narrow + step >= 0) & (narrow + step < narrow_size)

    def own_copies(act):
        for i, step in enumerate(own_steps):

            @pl.when(inside(step))
            def _():
                for p in range(len(spans)):
                    act(block_copy(narrow, p, gather_send_sem.at[i, p], step))

    def forward_copies(act, p):
        block = narrow_peer(reach)
        for distance in range(1, narrow_size - reach):
            for sign in (1, -1):
                below = narrow > block if sign > 0 else narrow < block

                @pl.when(below & inside(sign * distance))
                def _():
                    act(block_copy(block, p, forward_send_sem.at[distance - 1, p], sign * distance))

    own_copies(lambda copy: copy.start())

    def prepare_target(g, carry):
        for u in range(UNROLL):
            c = g * UNROLL + u
            x = padded(target_ref[:, pl.ds(pl.multiple_of(c * TILE, TILE), TILE)])
            first, second, third = split_three(x)
            right[c, 0:PAD, :] = first
            right[c, PAD : 2 * PAD, :] = second
            right[c, 2 * PAD : 3 * PAD, :] = third
            target_norm[pl.ds(c, 1), :] = jnp.sum(x * x, axis=0, keepdims=True) * norm_scale
        return carry

    for q in range(CHUNKS):
        loads[q + 1].wait()
        lax.fori_loop(
            q * chunk_tiles // UNROLL, (q + 1) * chunk_tiles // UNROLL, prepare_target, 0
        )
    for load in loads[CHUNKS + 1 :]:
        load.wait()

    lane = lax.broadcasted_iota(jnp.int32, (1, TILE), 1)

    def product_tile(p, r, q, x, beside):
        source_norm[pl.ds(q, 1), :] = jnp.sum(x * x, axis=0, keepdims=True) * norm_scale
        first, second, third = split_three(x * product_scale)
        leading = jnp.transpose(jnp.concatenate([first, second], axis=0))
        trailing = jnp.transpose(jnp.concatenate([first, third], axis=0))
        a = jnp.concatenate([leading, leading, trailing], axis=1)
        marks = []
        for k in range(0, K_MAX, 2):
            pair = []
            for j in (k, k + 1):
                c = cols_ref[j, r]
                first_part = right[c, 0:PAD, :]
                second_part = right[c, PAD : 2 * PAD, :]
                third_part = right[c, 2 * PAD : 3 * PAD, :]
                pair.append(
                    jnp.concatenate(
                        [first_part, first_part, second_part, second_part, third_part, first_part],
                        axis=0,
                    )
                )
                alive = j < counts_ref[0, r]
                marks.append((lane == jnp.where(alive, c, -1)).astype(jnp.float32))
            product = jnp.dot(
                a, jnp.concatenate(pair, axis=1), preferred_element_type=jnp.float32
            )
            beside(k * slabs // K_MAX, (k + 2) * slabs // K_MAX)
            for j in (k, k + 1):
                scores[p * K_MAX + j] = product[:, (j - k) * TILE : (j - k + 1) * TILE]
        marks = jnp.concatenate(marks, axis=0)
        one_hot[p * K_MAX : (p + 1) * K_MAX, :] = marks
        unmarked = 1.0 - jnp.sum(marks, axis=0, keepdims=True)
        marked[p] = jnp.concatenate(
            [marks, marks, unmarked, jnp.zeros((2 * K_MAX - 1, TILE), jnp.float32)], axis=0
        ).astype(jnp.bfloat16)

    def row_work(p, r, q):
        values, peaks, masses = [], [], []

        def some_slabs(low, high):
            if low == 0:
                for k in range(K_MAX):
                    value = jnp.where(
                        k < counts_ref[0, r], -target_norm[pl.ds(cols_ref[k, r], 1), :], very_low
                    )
                    values.append(jnp.broadcast_to(value, (SLAB, TILE)))
            for h in range(low, high):
                rows = slice(h * SLAB, (h + 1) * SLAB)
                s = [scores[p * K_MAX + k, rows, :] + values[k] for k in range(K_MAX)]
                top = tree(jnp.maximum, s)
                masses.append(tree(jnp.add, [jnp.exp2(x - top) for x in s]))
                peaks.append(top)
            if high == slabs:
                turned = jnp.transpose(jnp.concatenate(peaks, axis=0))
                total = jnp.transpose(jnp.concatenate(masses, axis=0))
                peak = jnp.max(turned, axis=0, keepdims=True)
                mass = jnp.sum(total * jnp.exp2(turned - peak), axis=0, keepdims=True)
                row_send[0, pl.ds(q, 1), :] = peak + log2(mass)

        return some_slabs

    half, quarter = narrow_size // 2, narrow_size // 4

    def crossed(d):
        return d // half % 2 != d // quarter % 2

    near = [d for d in range(1, narrow_size) if not crossed(d)]
    far = [d for d in range(1, narrow_size) if crossed(d) and d != reach]
    inner = (narrow >= quarter) & (narrow < narrow_size - quarter)
    early = 2 + len(near)

    def block_at(i):
        if i < 2:
            return narrow_peer(reach) if i else narrow
        first_choice, second_choice = (near + far)[i - 2], (far + near)[i - 2]
        return jnp.where(inner, narrow_peer(first_choice), narrow_peer(second_choice))

    def position_of(z):
        d = narrow_peer(z)
        position = jnp.where(d == reach, 1, 0)
        for i in range(2, narrow_size):
            chosen = jnp.where(inner, (near + far)[i - 2], (far + near)[i - 2])
            position = jnp.where(d == chosen, i, position)
        return position

    def place_of(z):
        outer = jnp.where(z < quarter, z + half, z)
        return jnp.where((z >= quarter) & (z < narrow_size - quarter), z - quarter, outer)

    order = list(range(quarter, narrow_size - quarter))
    order += list(range(quarter)) + list(range(narrow_size - quarter, narrow_size))

    def nothing(low, high):
        pass

    def products(positions):
        beside = nothing
        for i in positions:
            z = block_at(i)
            q = place_of(z) * shard_tiles
            for p in range(len(spans)):
                if i > 0:
                    block_copy(z, p, gather_send_sem.at[0, p], z - narrow).wait_recv()
                if i == 1:
                    forward_copies(lambda copy: copy.start(), p)
                for t in range(p * per_piece, (p + 1) * per_piece):
                    x = padded(
                        jnp.concatenate(
                            [
                                gathered[z, extra + t * full : extra + (t + 1) * full, :],
                                gathered[z, t * rest : (t + 1) * rest, :],
                            ],
                            axis=0,
                        )
                    )
                    here = (i * shard_tiles + t, z * shard_tiles + t, q + t)
                    product_tile(*here, x, beside)
                    beside = row_work(*here)
        beside(0, slabs)

    def exchange(axis_size, peer, where, src_of, buffer, me, send_sem, recv_sem):
        for d in range(1, axis_size):
            to = peer(d)
            remote(src_of(to), buffer.at[me], send_sem, recv_sem, where(to)).start()

        def finish():
            everything = buffer.at[0 : axis_size - 1]
            whole = remote(everything, everything, send_sem, recv_sem, where(peer(1)))
            whole.wait_recv()
            whole.wait_send()

        return finish

    part_rows = row_count // PARTS
    edge = part_rows // 2

    def row_share(step, part):
        rows = slice(part * part_rows, (part + 1) * part_rows)
        row_recv[step, narrow, rows, :] = row_send[step, rows, :]
        return exchange(
            narrow_size,
            narrow_peer,
            at_narrow,
            lambda to: row_send.at[step, rows],
            row_recv.at[step, :, rows],
            narrow,
            row_send_sem.at[step, part],
            row_recv_sem.at[step, part],
        )

    def row_combine(step, part):
        rows = slice(part * part_rows, (part + 1) * part_rows)
        parts = [row_recv[step, z, rows, :] for z in range(narrow_size)]
        if part == 0:
            mass = row_mass_ref[edge : row_count - edge, :]
        else:
            mass = jnp.concatenate(
                [row_mass_ref[0:edge, :], row_mass_ref[row_count - edge : row_count, :]], axis=0
            )
        if step == 0:
            top = functools.reduce(jnp.maximum, parts)
            total = sum(jnp.exp2(p - top) for p in parts)
            row_values[rows, :] = log2(mass) - (top + log2(total))
            return
        total = sum(parts)
        row_factor[rows, :] = mass / total
        result = potential_scale * (
            row_values[rows, :] + log2(mass) - log2(total) + source_norm[rows, :]
        )
        if part == 0:
            row_out_ref[edge : row_count - edge, :] = result
        else:
            row_out_ref[0:edge, :] = result[0:edge]
            row_out_ref[row_count - edge : row_count, :] = result[edge:]

    def spread_rows(ref, r):
        return jnp.transpose(jnp.broadcast_to(ref[pl.ds(r, 1), :], (TILE, TILE)))

    def first_col_tile(p, r, q):
        values = spread_rows(row_values, q)
        peaks, masses = [], []
        for k in range(K_MAX):
            slot = p * K_MAX + k
            s = [
                scores[slot, h * SLAB : (h + 1) * SLAB, :] + values[h * SLAB : (h + 1) * SLAB]
                for h in range(slabs)
            ]
            top = tree(jnp.maximum, s)
            terms = [jnp.exp2(x - top) for x in s]
            for h in range(slabs):
                scores[slot, h * SLAB : (h + 1) * SLAB, :] = terms[h]
            total = tree(jnp.add, terms)
            peak = jnp.max(top, axis=0, keepdims=True)
            masses.append(jnp.sum(total * jnp.exp2(top - peak), axis=0, keepdims=True))
            alive = k < counts_ref[0, r]
            tops[slot] = jnp.where(alive, top, very_low)
            peaks.append(jnp.where(alive, peak, very_low))
        place = pl.ds(pl.multiple_of(p * K_MAX, K_MAX), K_MAX)
        slot_peak[place, :] = jnp.concatenate(peaks, axis=0)
        slot_mass[place, :] = jnp.concatenate(masses, axis=0)

    def second_row_tile(p, r, q):
        total = [None] * slabs
        for k in range(K_MAX):
            slot = p * K_MAX + k
            factor = jnp.exp2(
                tops[slot]
                + jnp.broadcast_to(col_values[pl.ds(cols_ref[k, r], 1), :], (SLAB, TILE))
            )
            tops[slot] = factor
            for h in range(slabs):
                term = scores[slot, h * SLAB : (h + 1) * SLAB, :] * factor
                total[h] = term if k == 0 else total[h] + term
        turned = jnp.transpose(jnp.concatenate(total, axis=0))
        row_send[1, pl.ds(q, 1), :] = jnp.sum(turned, axis=0, keepdims=True)

    def second_col_tile(p, r, q):
        values = spread_rows(row_factor, q)
        masses = []
        for k in range(K_MAX):
            slot = p * K_MAX + k
            total = tree(
                jnp.add,
                [
                    scores[slot, h * SLAB : (h + 1) * SLAB, :] * values[h * SLAB : (h + 1) * SLAB]
                    for h in range(slabs)
                ],
            )
            masses.append(jnp.sum(total * tops[slot], axis=0, keepdims=True))
        place = pl.ds(pl.multiple_of(p * K_MAX, K_MAX), K_MAX)
        slot_mass[place, :] = jnp.concatenate(masses, axis=0)

    def over_tiles(part, one_tile):
        together = min(COL_UNROLL, shard_tiles)
        for i in range(part * half, (part + 1) * half):
            z = order[i]
            position = position_of(z)

            def some(g, carry):
                for u in range(together):
                    t = g * together + u
                    one_tile(
                        position * shard_tiles + t, z * shard_tiles + t, i * shard_tiles + t
                    )
                return carry

            lax.fori_loop(0, shard_tiles // together, some, 0)

    def split_two(x, axis):
        coarse = x.astype(jnp.bfloat16)
        fine = (x - coarse.astype(jnp.float32)).astype(jnp.bfloat16)
        return jnp.concatenate([coarse, fine], axis=axis)

    def column_sums(x):
        return jnp.dot(
            one_hot_cols[...], split_two(x, 0), preferred_element_type=jnp.float32
        )

    def column_lse():
        high = None
        for r in range(row_count):
            peaks = slot_peak[r * K_MAX : (r + 1) * K_MAX, :]
            coarse = peaks.astype(jnp.bfloat16).astype(jnp.float32)
            stack = jnp.concatenate(
                [
                    coarse,
                    peaks - coarse,
                    jnp.full((1, TILE), very_low, jnp.float32),
                    jnp.zeros((2 * K_MAX - 1, TILE), jnp.float32),
                ],
                axis=0,
            ).astype(jnp.bfloat16)
            spread = lax.dot_general(
                marked[r],
                stack,
                (((0,), (0,)), ((), ())),
                preferred_element_type=jnp.float32,
            )
            high = spread if high is None else jnp.maximum(high, spread)
        found = jnp.dot(
            one_hot_rows[...], split_two(high, 1), preferred_element_type=jnp.float32
        )
        found = found[:, 0:TILE] + found[:, TILE : 2 * TILE]
        summed = column_sums(slot_mass[...] * jnp.exp2(jnp.minimum(slot_peak[...] - found, 1e2)))
        return jnp.where(summed > 0.0, high + log2(jnp.maximum(summed, 1e-30)), very_low)

    def columns_share(step, sums):
        for w in range(wide_size):
            col_send[step, w] = sums[w * piece : (w + 1) * piece]
        finish = exchange(
            wide_size,
            wide_peer,
            at_wide,
            lambda to: col_send.at[step, to],
            col_recv.at[step],
            wide,
            scatter_send_sem.at[step],
            scatter_recv_sem.at[step],
        )
        col_recv[step, wide] = col_send[step, wide]
        finish()
        parts = [col_recv[step, w] for w in range(wide_size)]
        rows = pl.ds(pl.multiple_of(wide * piece, piece), piece)
        mass = col_mass_ref[rows, :]
        if step == 0:
            top = tree(jnp.maximum, parts)
            total = tree(jnp.add, [jnp.exp2(p - top) for p in parts])
            col_pieces[step, wide] = log2(mass) - (top + log2(total))
        else:
            total = tree(jnp.add, parts)
            col_pieces[step, wide] = potential_scale * (
                col_values[rows, :] + log2(mass) - log2(total) + target_norm[rows, :]
            )
        finish = exchange(
            wide_size,
            wide_peer,
            at_wide,
            lambda to: col_pieces.at[step, wide],
            col_pieces.at[step],
            wide,
            spread_send_sem.at[step],
            spread_recv_sem.at[step],
        )
        finish()
        where = col_values if step == 0 else col_out_ref
        for w in range(wide_size):
            where[w * piece : (w + 1) * piece, :] = col_pieces[step, w]

    products(range(early))
    finishes = [row_share(0, 0)]
    products(range(early, narrow_size))
    finishes.append(row_share(0, 1))
    one_hot_rows[...] = one_hot[...].astype(jnp.bfloat16)
    turned = jnp.transpose(one_hot[...]).astype(jnp.bfloat16)
    one_hot_cols[...] = jnp.concatenate([turned, turned], axis=1)
    own_copies(lambda copy: copy.wait_send())
    for p in range(len(spans)):
        forward_copies(lambda copy: copy.wait_send(), p)
    for part in range(PARTS):
        finishes[part]()
        row_combine(0, part)
        over_tiles(part, first_col_tile)
    columns_share(0, column_lse())

    finishes = []
    for part in range(PARTS):
        over_tiles(part, second_row_tile)
        finishes.append(row_share(1, part))
    for part in range(PARTS):
        finishes[part]()
        row_combine(1, part)
        over_tiles(part, second_col_tile)
    columns_share(1, column_sums(slot_mass[...]))


def hand_over(rows_ref, cols_ref, rows_out_ref, cols_out_ref):
    rows_out_ref[...] = rows_ref[...]
    cols_out_ref[...] = cols_ref[...]


def local(
    wide_size,
    narrow_size,
    source_features,
    target_features,
    source_mass,
    target_mass,
    block_cols,
    block_counts,
):
    row_count = source_mass.shape[0] // TILE
    col_count = target_mass.shape[0] // TILE
    slots = row_count * K_MAX
    piece = col_count // wide_size
    spans = packing(row_count // narrow_size)[-1]
    reach = max(1, narrow_size // 2)
    vmem = pl.BlockSpec(memory_space=pltpu.VMEM)
    hbm = pl.BlockSpec(memory_space=pltpu.HBM)
    f32 = jnp.float32
    bf16 = jnp.bfloat16
    dma = pltpu.SemaphoreType.DMA
    rows, cols = pl.pallas_call(
        functools.partial(kernel, wide_size, narrow_size),
        out_shape=(
            jax.ShapeDtypeStruct((row_count, TILE), f32),
            jax.ShapeDtypeStruct((col_count, TILE), f32),
        ),
        in_specs=[hbm] * 6,
        out_specs=(vmem, vmem),
        scratch_shapes=[
            pltpu.SMEM((K_MAX, row_count), jnp.int32),
            pltpu.SMEM((1, row_count), jnp.int32),
            pltpu.VMEM(source_features.shape, f32),
            pltpu.VMEM((narrow_size, spans[-1][1], TILE), f32),
            pltpu.VMEM(target_features.shape, f32),
            pltpu.VMEM((row_count, TILE), f32),
            pltpu.VMEM((col_count, TILE), f32),
            pltpu.VMEM((col_count, 3 * PAD, TILE), bf16),
            pltpu.VMEM((slots, TILE, TILE), f32),
            pltpu.VMEM((slots, col_count), f32),
            pltpu.VMEM((slots, col_count), bf16),
            pltpu.VMEM((col_count, 2 * slots), bf16),
            pltpu.VMEM((row_count, 4 * K_MAX, col_count), bf16),
            pltpu.VMEM((row_count, TILE), f32),
            pltpu.VMEM((col_count, TILE), f32),
            pltpu.VMEM((col_count, TILE), f32),
            pltpu.VMEM((ITERS, wide_size, piece, TILE), f32),
            pltpu.VMEM((row_count, TILE), f32),
            pltpu.VMEM((row_count, TILE), f32),
            pltpu.VMEM((ITERS, row_count, TILE), f32),
            pltpu.VMEM((ITERS, narrow_size, row_count, TILE), f32),
            pltpu.VMEM((slots, SLAB, TILE), f32),
            pltpu.VMEM((slots, TILE), f32),
            pltpu.VMEM((slots, TILE), f32),
            pltpu.VMEM((ITERS, wide_size, piece, TILE), f32),
            pltpu.VMEM((ITERS, wide_size, piece, TILE), f32),
            dma((CHUNKS + 5,)),
            dma((2 * reach, len(spans))),
            dma((max(1, narrow_size - 1 - reach), len(spans))),
            dma((narrow_size, len(spans))),
            dma((ITERS, PARTS)),
            dma((ITERS, PARTS)),
            dma((ITERS,)),
            dma((ITERS,)),
            dma((ITERS,)),
            dma((ITERS,)),
        ],
        compiler_params=pltpu.CompilerParams(
            collective_id=0, has_side_effects=True, vmem_limit_bytes=67043328
        ),
    )(
        block_cols.T,
        block_counts.T,
        source_features,
        target_features,
        source_mass.reshape(row_count, TILE),
        target_mass.reshape(col_count, TILE),
    )
    rows, cols = pl.pallas_call(
        hand_over,
        out_shape=(
            jax.ShapeDtypeStruct((row_count, TILE), f32),
            jax.ShapeDtypeStruct((col_count, TILE), f32),
        ),
        in_specs=[vmem, vmem],
        out_specs=(vmem, vmem),
    )(rows, cols)
    return rows.reshape(-1), cols.reshape(-1)


def solution(mesh):
    in_specs = (
        P(None, ("wide", "narrow")),
        P(None, "narrow"),
        P("wide"),
        P("narrow"),
        P("wide", "narrow"),
        P("wide", "narrow"),
    )
    out_specs = (P("wide"), P("narrow"))
    return jax.shard_map(
        functools.partial(local, mesh.shape["wide"], mesh.shape["narrow"]),
        mesh=mesh,
        in_specs=in_specs,
        out_specs=out_specs,
        check_vma=False,
    )
```

```python
import functools

import jax
import jax.numpy as jnp
from jax import lax
from jax.experimental import pallas as pl
from jax.experimental.pallas import tpu as pltpu
from jax.sharding import PartitionSpec as P

F = 50
TILE = 128
K_MAX = 8
ITERS = 2
PAD = 64
CHUNKS = 4
SLAB = 8
UNROLL = 4
COL_UNROLL = 2
PARTS = 2

epsilon = 0.05
very_low = -1e30
log2_e = 1.4426950408889634
product_scale = 2.0 * log2_e / (F * epsilon)
norm_scale = log2_e / (F * epsilon)
potential_scale = epsilon / log2_e


def split_three(x):
    first = x.astype(jnp.bfloat16)
    rest = x - first.astype(jnp.float32)
    second = rest.astype(jnp.bfloat16)
    third = (rest - second.astype(jnp.float32)).astype(jnp.bfloat16)
    return first, second, third


def log2(x):
    return jnp.log(x) * log2_e


def paired(me, d, size):
    other, bit = 0, 1
    while bit < size:
        other = other + lax.rem(lax.div(me, bit) + d // bit % 2, 2) * bit
        bit *= 2
    return other


def tree(combine, parts):
    parts = list(parts)
    while len(parts) > 1:
        pairs = [combine(a, b) for a, b in zip(parts[0::2], parts[1::2])]
        parts = pairs + parts[len(parts) // 2 * 2 :]
    return parts[0]


def padded(x):
    return jnp.concatenate([x, jnp.zeros((PAD - F, TILE), jnp.float32)], axis=0)


def packing(shard_tiles):
    rest = F % SLAB
    extra = -(-shard_tiles * rest // SLAB) * SLAB
    full = F - rest
    pieces = 2 if shard_tiles % 2 == 0 else 1
    per_piece = shard_tiles // pieces
    ends = [extra + (p + 1) * per_piece * full for p in range(pieces)]
    return rest, extra, full, per_piece, list(zip([0] + ends[:-1], ends))


def kernel(
    wide_size,
    narrow_size,
    cols_hbm,
    counts_hbm,
    source_hbm,
    target_hbm,
    row_mass_hbm,
    col_mass_hbm,
    row_out_hbm,
    col_out_hbm,
    row_out_ref,
    cols_ref,
    counts_ref,
    source_ref,
    gathered,
    target_ref,
    row_mass_ref,
    col_mass_ref,
    right,
    scores,
    one_hot,
    one_hot_rows,
    one_hot_cols,
    marked,
    source_norm,
    target_norm,
    col_values,
    col_pieces,
    row_values,
    row_factor,
    row_send,
    row_recv,
    tops,
    slot_peak,
    slot_mass,
    col_send,
    col_recv,
    load_sem,
    out_sem,
    gather_send_sem,
    forward_send_sem,
    gather_recv_sem,
    row_send_sem,
    row_recv_sem,
    scatter_send_sem,
    scatter_recv_sem,
    spread_send_sem,
    spread_recv_sem,
):
    wide = lax.axis_index("wide")
    narrow = lax.axis_index("narrow")
    row_count = row_mass_ref.shape[0]
    col_count = col_mass_ref.shape[0]
    shard_tiles = row_count // narrow_size
    piece = col_count // wide_size
    chunk_tiles = col_count // CHUNKS
    chunk_cols = chunk_tiles * TILE
    slabs = TILE // SLAB
    rest, extra, full, per_piece, spans = packing(shard_tiles)
    reach = max(1, narrow_size // 2)

    def wide_peer(d):
        return paired(wide, d, wide_size)

    def narrow_peer(d):
        return paired(narrow, d, narrow_size)

    def at_wide(w):
        return {"wide": w, "narrow": narrow}

    def at_narrow(z):
        return {"wide": wide, "narrow": z}

    def remote(src, dst, send, recv, where):
        return pltpu.make_async_remote_copy(
            src_ref=src,
            dst_ref=dst,
            send_sem=send,
            recv_sem=recv,
            device_id=where,
            device_id_type=pl.DeviceIdType.MESH,
        )

    barrier = pltpu.get_barrier_semaphore()
    for d in range(1, narrow_size):
        pl.semaphore_signal(
            barrier, inc=1, device_id=at_narrow(narrow_peer(d)), device_id_type=pl.DeviceIdType.MESH
        )
    for d in range(1, wide_size):
        pl.semaphore_signal(
            barrier, inc=1, device_id=at_wide(wide_peer(d)), device_id_type=pl.DeviceIdType.MESH
        )
    loads = [pltpu.make_async_copy(source_hbm, source_ref, load_sem.at[CHUNKS])]
    for q in range(CHUNKS):
        part = pl.ds(q * chunk_cols, chunk_cols)
        loads.append(
            pltpu.make_async_copy(target_hbm.at[:, part], target_ref.at[:, part], load_sem.at[q])
        )
    loads.append(pltpu.make_async_copy(row_mass_hbm, row_mass_ref, load_sem.at[CHUNKS + 1]))
    loads.append(pltpu.make_async_copy(col_mass_hbm, col_mass_ref, load_sem.at[CHUNKS + 2]))
    loads.append(pltpu.make_async_copy(cols_hbm, cols_ref, load_sem.at[CHUNKS + 3]))
    loads.append(pltpu.make_async_copy(counts_hbm, counts_ref, load_sem.at[CHUNKS + 4]))
    for load in loads:
        load.start()

    loads[0].wait()
    tiles = [slice(t * TILE, (t + 1) * TILE) for t in range(shard_tiles)]
    left = [source_ref[full:F, tile] for tile in tiles]
    fill = extra - rest * shard_tiles
    if fill:
        left.append(jnp.zeros((fill, TILE), jnp.float32))
    gathered[narrow, 0:extra, :] = jnp.concatenate(left, axis=0)
    for t, tile in enumerate(tiles):
        gathered[narrow, extra + t * full : extra + (t + 1) * full, :] = source_ref[0:full, tile]
    pl.semaphore_wait(barrier, narrow_size + wide_size - 2)

    def block_copy(block, p, send, step):
        part = gathered.at[block, spans[p][0] : spans[p][1]]
        return remote(part, part, send, gather_recv_sem.at[block, p], at_narrow(narrow + step))

    own_steps = [
        sign * distance
        for distance in [reach] + list(range(1, reach))
        for sign in (1, -1)
    ]

    def inside(step):
        return (narrow + step >= 0) & (narrow + step < narrow_size)

    def own_copies(act):
        for i, step in enumerate(own_steps):

            @pl.when(inside(step))
            def _():
                for p in range(len(spans)):
                    act(block_copy(narrow, p, gather_send_sem.at[i, p], step))

    def forward_copies(act, p):
        block = narrow_peer(reach)
        for distance in range(1, narrow_size - reach):
            for sign in (1, -1):
                below = narrow > block if sign > 0 else narrow < block

                @pl.when(below & inside(sign * distance))
                def _():
                    act(block_copy(block, p, forward_send_sem.at[distance - 1, p], sign * distance))

    own_copies(lambda copy: copy.start())

    def prepare_target(g, carry):
        for u in range(UNROLL):
            c = g * UNROLL + u
            x = padded(target_ref[:, pl.ds(pl.multiple_of(c * TILE, TILE), TILE)])
            first, second, third = split_three(x)
            right[c, 0:PAD, :] = first
            right[c, PAD : 2 * PAD, :] = second
            right[c, 2 * PAD : 3 * PAD, :] = third
            target_norm[pl.ds(c, 1), :] = jnp.sum(x * x, axis=0, keepdims=True) * norm_scale
        return carry

    for q in range(CHUNKS):
        loads[q + 1].wait()
        lax.fori_loop(
            q * chunk_tiles // UNROLL, (q + 1) * chunk_tiles // UNROLL, prepare_target, 0
        )
    for load in loads[CHUNKS + 1 :]:
        load.wait()

    lane = lax.broadcasted_iota(jnp.int32, (1, TILE), 1)

    def product_tile(p, r, q, x, beside):
        source_norm[pl.ds(q, 1), :] = jnp.sum(x * x, axis=0, keepdims=True) * norm_scale
        first, second, third = split_three(x * product_scale)
        leading = jnp.transpose(jnp.concatenate([first, second], axis=0))
        trailing = jnp.transpose(jnp.concatenate([first, third], axis=0))
        a = jnp.concatenate([leading, leading, trailing], axis=1)
        marks = []
        for k in range(0, K_MAX, 2):
            pair = []
            for j in (k, k + 1):
                c = cols_ref[j, r]
                first_part = right[c, 0:PAD, :]
                second_part = right[c, PAD : 2 * PAD, :]
                third_part = right[c, 2 * PAD : 3 * PAD, :]
                pair.append(
                    jnp.concatenate(
                        [first_part, first_part, second_part, second_part, third_part, first_part],
                        axis=0,
                    )
                )
                alive = j < counts_ref[0, r]
                marks.append((lane == jnp.where(alive, c, -1)).astype(jnp.float32))
            product = jnp.dot(
                a, jnp.concatenate(pair, axis=1), preferred_element_type=jnp.float32
            )
            beside(k * slabs // K_MAX, (k + 2) * slabs // K_MAX)
            for j in (k, k + 1):
                scores[p * K_MAX + j] = product[:, (j - k) * TILE : (j - k + 1) * TILE]
        marks = jnp.concatenate(marks, axis=0)
        one_hot[p * K_MAX : (p + 1) * K_MAX, :] = marks
        unmarked = 1.0 - jnp.sum(marks, axis=0, keepdims=True)
        marked[p] = jnp.concatenate(
            [marks, marks, unmarked, jnp.zeros((2 * K_MAX - 1, TILE), jnp.float32)], axis=0
        ).astype(jnp.bfloat16)

    def row_work(p, r, q):
        values, peaks, masses = [], [], []

        def some_slabs(low, high):
            if low == 0:
                for k in range(K_MAX):
                    value = jnp.where(
                        k < counts_ref[0, r], -target_norm[pl.ds(cols_ref[k, r], 1), :], very_low
                    )
                    values.append(jnp.broadcast_to(value, (SLAB, TILE)))
            for h in range(low, high):
                rows = slice(h * SLAB, (h + 1) * SLAB)
                s = [scores[p * K_MAX + k, rows, :] + values[k] for k in range(K_MAX)]
                top = tree(jnp.maximum, s)
                masses.append(tree(jnp.add, [jnp.exp2(x - top) for x in s]))
                peaks.append(top)
            if high == slabs:
                turned = jnp.transpose(jnp.concatenate(peaks, axis=0))
                total = jnp.transpose(jnp.concatenate(masses, axis=0))
                peak = jnp.max(turned, axis=0, keepdims=True)
                mass = jnp.sum(total * jnp.exp2(turned - peak), axis=0, keepdims=True)
                row_send[0, pl.ds(q, 1), :] = peak + log2(mass)

        return some_slabs

    half, quarter = narrow_size // 2, narrow_size // 4

    def crossed(d):
        return d // half % 2 != d // quarter % 2

    near = [d for d in range(1, narrow_size) if not crossed(d)]
    far = [d for d in range(1, narrow_size) if crossed(d) and d != reach]
    inner = (narrow >= quarter) & (narrow < narrow_size - quarter)
    early = 2 + len(near)

    def block_at(i):
        if i < 2:
            return narrow_peer(reach) if i else narrow
        first_choice, second_choice = (near + far)[i - 2], (far + near)[i - 2]
        return jnp.where(inner, narrow_peer(first_choice), narrow_peer(second_choice))

    def position_of(z):
        d = narrow_peer(z)
        position = jnp.where(d == reach, 1, 0)
        for i in range(2, narrow_size):
            chosen = jnp.where(inner, (near + far)[i - 2], (far + near)[i - 2])
            position = jnp.where(d == chosen, i, position)
        return position

    def place_of(z):
        outer = jnp.where(z < quarter, z + half, z)
        return jnp.where((z >= quarter) & (z < narrow_size - quarter), z - quarter, outer)

    order = list(range(quarter, narrow_size - quarter))
    order += list(range(quarter)) + list(range(narrow_size - quarter, narrow_size))

    def nothing(low, high):
        pass

    def products(positions):
        beside = nothing
        for i in positions:
            z = block_at(i)
            q = place_of(z) * shard_tiles
            for p in range(len(spans)):
                if i > 0:
                    block_copy(z, p, gather_send_sem.at[0, p], z - narrow).wait_recv()
                if i == 1:
                    forward_copies(lambda copy: copy.start(), p)
                for t in range(p * per_piece, (p + 1) * per_piece):
                    x = padded(
                        jnp.concatenate(
                            [
                                gathered[z, extra + t * full : extra + (t + 1) * full, :],
                                gathered[z, t * rest : (t + 1) * rest, :],
                            ],
                            axis=0,
                        )
                    )
                    here = (i * shard_tiles + t, z * shard_tiles + t, q + t)
                    product_tile(*here, x, beside)
                    beside = row_work(*here)
        beside(0, slabs)

    def exchange(axis_size, peer, where, src_of, buffer, me, send_sem, recv_sem):
        for d in range(1, axis_size):
            to = peer(d)
            remote(src_of(to), buffer.at[me], send_sem, recv_sem, where(to)).start()

        def finish():
            everything = buffer.at[0 : axis_size - 1]
            whole = remote(everything, everything, send_sem, recv_sem, where(peer(1)))
            whole.wait_recv()
            whole.wait_send()

        return finish

    part_rows = row_count // PARTS
    edge = part_rows // 2

    def row_share(step, part):
        rows = slice(part * part_rows, (part + 1) * part_rows)
        row_recv[step, narrow, rows, :] = row_send[step, rows, :]
        return exchange(
            narrow_size,
            narrow_peer,
            at_narrow,
            lambda to: row_send.at[step, rows],
            row_recv.at[step, :, rows],
            narrow,
            row_send_sem.at[step, part],
            row_recv_sem.at[step, part],
        )

    def row_combine(step, part):
        rows = slice(part * part_rows, (part + 1) * part_rows)
        parts = [row_recv[step, z, rows, :] for z in range(narrow_size)]
        if part == 0:
            mass = row_mass_ref[edge : row_count - edge, :]
        else:
            mass = jnp.concatenate(
                [row_mass_ref[0:edge, :], row_mass_ref[row_count - edge : row_count, :]], axis=0
            )
        if step == 0:
            top = functools.reduce(jnp.maximum, parts)
            total = sum(jnp.exp2(p - top) for p in parts)
            row_values[rows, :] = log2(mass) - (top + log2(total))
            return
        total = sum(parts)
        row_factor[rows, :] = mass / total
        result = potential_scale * (
            row_values[rows, :] + log2(mass) - log2(total) + source_norm[rows, :]
        )
        if part == 0:
            row_out_ref[edge : row_count - edge, :] = result
        else:
            row_out_ref[0:edge, :] = result[0:edge]
            row_out_ref[row_count - edge : row_count, :] = result[edge:]

    def spread_rows(ref, r):
        return jnp.transpose(jnp.broadcast_to(ref[pl.ds(r, 1), :], (TILE, TILE)))

    def first_col_tile(p, r, q):
        values = spread_rows(row_values, q)
        peaks, masses = [], []
        for k in range(K_MAX):
            slot = p * K_MAX + k
            s = [
                scores[slot, h * SLAB : (h + 1) * SLAB, :] + values[h * SLAB : (h + 1) * SLAB]
                for h in range(slabs)
            ]
            top = tree(jnp.maximum, s)
            terms = [jnp.exp2(x - top) for x in s]
            for h in range(slabs):
                scores[slot, h * SLAB : (h + 1) * SLAB, :] = terms[h]
            total = tree(jnp.add, terms)
            peak = jnp.max(top, axis=0, keepdims=True)
            masses.append(jnp.sum(total * jnp.exp2(top - peak), axis=0, keepdims=True))
            alive = k < counts_ref[0, r]
            tops[slot] = jnp.where(alive, top, very_low)
            peaks.append(jnp.where(alive, peak, very_low))
        place = pl.ds(pl.multiple_of(p * K_MAX, K_MAX), K_MAX)
        slot_peak[place, :] = jnp.concatenate(peaks, axis=0)
        slot_mass[place, :] = jnp.concatenate(masses, axis=0)

    def second_row_tile(p, r, q):
        total = [None] * slabs
        for k in range(K_MAX):
            slot = p * K_MAX + k
            factor = jnp.exp2(
                tops[slot]
                + jnp.broadcast_to(col_values[pl.ds(cols_ref[k, r], 1), :], (SLAB, TILE))
            )
            tops[slot] = factor
            for h in range(slabs):
                term = scores[slot, h * SLAB : (h + 1) * SLAB, :] * factor
                total[h] = term if k == 0 else total[h] + term
        turned = jnp.transpose(jnp.concatenate(total, axis=0))
        row_send[1, pl.ds(q, 1), :] = jnp.sum(turned, axis=0, keepdims=True)

    def second_col_tile(p, r, q):
        values = spread_rows(row_factor, q)
        masses = []
        for k in range(K_MAX):
            slot = p * K_MAX + k
            total = tree(
                jnp.add,
                [
                    scores[slot, h * SLAB : (h + 1) * SLAB, :] * values[h * SLAB : (h + 1) * SLAB]
                    for h in range(slabs)
                ],
            )
            masses.append(jnp.sum(total * tops[slot], axis=0, keepdims=True))
        place = pl.ds(pl.multiple_of(p * K_MAX, K_MAX), K_MAX)
        slot_mass[place, :] = jnp.concatenate(masses, axis=0)

    def over_tiles(part, one_tile):
        together = min(COL_UNROLL, shard_tiles)
        for i in range(part * half, (part + 1) * half):
            z = order[i]
            position = position_of(z)

            def some(g, carry):
                for u in range(together):
                    t = g * together + u
                    one_tile(
                        position * shard_tiles + t, z * shard_tiles + t, i * shard_tiles + t
                    )
                return carry

            lax.fori_loop(0, shard_tiles // together, some, 0)

    def split_two(x, axis):
        coarse = x.astype(jnp.bfloat16)
        fine = (x - coarse.astype(jnp.float32)).astype(jnp.bfloat16)
        return jnp.concatenate([coarse, fine], axis=axis)

    def column_sums(x):
        return jnp.dot(
            one_hot_cols[...], split_two(x, 0), preferred_element_type=jnp.float32
        )

    def column_lse():
        high = None
        for r in range(row_count):
            peaks = slot_peak[r * K_MAX : (r + 1) * K_MAX, :]
            coarse = peaks.astype(jnp.bfloat16).astype(jnp.float32)
            stack = jnp.concatenate(
                [
                    coarse,
                    peaks - coarse,
                    jnp.full((1, TILE), very_low, jnp.float32),
                    jnp.zeros((2 * K_MAX - 1, TILE), jnp.float32),
                ],
                axis=0,
            ).astype(jnp.bfloat16)
            spread = lax.dot_general(
                marked[r],
                stack,
                (((0,), (0,)), ((), ())),
                preferred_element_type=jnp.float32,
            )
            high = spread if high is None else jnp.maximum(high, spread)
        found = jnp.dot(
            one_hot_rows[...], split_two(high, 1), preferred_element_type=jnp.float32
        )
        found = found[:, 0:TILE] + found[:, TILE : 2 * TILE]
        summed = column_sums(slot_mass[...] * jnp.exp2(jnp.minimum(slot_peak[...] - found, 1e2)))
        return jnp.where(summed > 0.0, high + log2(jnp.maximum(summed, 1e-30)), very_low)

    def columns_share(step, sums):
        for w in range(wide_size):
            col_send[step, w] = sums[w * piece : (w + 1) * piece]
        finish = exchange(
            wide_size,
            wide_peer,
            at_wide,
            lambda to: col_send.at[step, to],
            col_recv.at[step],
            wide,
            scatter_send_sem.at[step],
            scatter_recv_sem.at[step],
        )
        col_recv[step, wide] = col_send[step, wide]
        finish()
        parts = [col_recv[step, w] for w in range(wide_size)]
        rows = pl.ds(pl.multiple_of(wide * piece, piece), piece)
        mass = col_mass_ref[rows, :]
        if step == 0:
            top = tree(jnp.maximum, parts)
            total = tree(jnp.add, [jnp.exp2(p - top) for p in parts])
            col_pieces[step, wide] = log2(mass) - (top + log2(total))
        else:
            total = tree(jnp.add, parts)
            col_pieces[step, wide] = potential_scale * (
                col_values[rows, :] + log2(mass) - log2(total) + target_norm[rows, :]
            )
        finish = exchange(
            wide_size,
            wide_peer,
            at_wide,
            lambda to: col_pieces.at[step, wide],
            col_pieces.at[step] if step == 0 else col_out_hbm,
            wide,
            spread_send_sem.at[step],
            spread_recv_sem.at[step],
        )
        if step == 0:
            finish()
            for w in range(wide_size):
                col_values[w * piece : (w + 1) * piece, :] = col_pieces[step, w]
            return
        keep = pltpu.make_async_copy(
            col_pieces.at[step, wide], col_out_hbm.at[wide], out_sem.at[1]
        )
        keep.start()
        keep.wait()
        finish()

    products(range(early))
    finishes = [row_share(0, 0)]
    products(range(early, narrow_size))
    finishes.append(row_share(0, 1))
    one_hot_rows[...] = one_hot[...].astype(jnp.bfloat16)
    turned = jnp.transpose(one_hot[...]).astype(jnp.bfloat16)
    one_hot_cols[...] = jnp.concatenate([turned, turned], axis=1)
    own_copies(lambda copy: copy.wait_send())
    for p in range(len(spans)):
        forward_copies(lambda copy: copy.wait_send(), p)
    for part in range(PARTS):
        finishes[part]()
        row_combine(0, part)
        over_tiles(part, first_col_tile)
    columns_share(0, column_lse())

    finishes = []
    for part in range(PARTS):
        over_tiles(part, second_row_tile)
        finishes.append(row_share(1, part))
    for part in range(PARTS):
        finishes[part]()
        row_combine(1, part)
        over_tiles(part, second_col_tile)
    rows_out = pltpu.make_async_copy(row_out_ref, row_out_hbm, out_sem.at[0])
    rows_out.start()
    columns_share(1, column_sums(slot_mass[...]))
    rows_out.wait()


def hand_over(rows_ref, cols_ref, rows_out_ref, cols_out_ref):
    rows_out_ref[...] = rows_ref[...]
    piece = cols_ref.shape[1]
    for w in range(cols_ref.shape[0]):
        cols_out_ref[w * piece : (w + 1) * piece, :] = cols_ref[w]


def local(
    wide_size,
    narrow_size,
    source_features,
    target_features,
    source_mass,
    target_mass,
    block_cols,
    block_counts,
):
    row_count = source_mass.shape[0] // TILE
    col_count = target_mass.shape[0] // TILE
    slots = row_count * K_MAX
    piece = col_count // wide_size
    spans = packing(row_count // narrow_size)[-1]
    reach = max(1, narrow_size // 2)
    vmem = pl.BlockSpec(memory_space=pltpu.VMEM)
    hbm = pl.BlockSpec(memory_space=pltpu.HBM)
    f32 = jnp.float32
    bf16 = jnp.bfloat16
    dma = pltpu.SemaphoreType.DMA
    rows, cols = pl.pallas_call(
        functools.partial(kernel, wide_size, narrow_size),
        out_shape=(
            jax.ShapeDtypeStruct((row_count, TILE), f32),
            jax.ShapeDtypeStruct((wide_size, piece, TILE), f32),
        ),
        in_specs=[hbm] * 6,
        out_specs=(hbm, hbm),
        scratch_shapes=[
            pltpu.VMEM((row_count, TILE), f32),
            pltpu.SMEM((K_MAX, row_count), jnp.int32),
            pltpu.SMEM((1, row_count), jnp.int32),
            pltpu.VMEM(source_features.shape, f32),
            pltpu.VMEM((narrow_size, spans[-1][1], TILE), f32),
            pltpu.VMEM(target_features.shape, f32),
            pltpu.VMEM((row_count, TILE), f32),
            pltpu.VMEM((col_count, TILE), f32),
            pltpu.VMEM((col_count, 3 * PAD, TILE), bf16),
            pltpu.VMEM((slots, TILE, TILE), f32),
            pltpu.VMEM((slots, col_count), f32),
            pltpu.VMEM((slots, col_count), bf16),
            pltpu.VMEM((col_count, 2 * slots), bf16),
            pltpu.VMEM((row_count, 4 * K_MAX, col_count), bf16),
            pltpu.VMEM((row_count, TILE), f32),
            pltpu.VMEM((col_count, TILE), f32),
            pltpu.VMEM((col_count, TILE), f32),
            pltpu.VMEM((ITERS, wide_size, piece, TILE), f32),
            pltpu.VMEM((row_count, TILE), f32),
            pltpu.VMEM((row_count, TILE), f32),
            pltpu.VMEM((ITERS, row_count, TILE), f32),
            pltpu.VMEM((ITERS, narrow_size, row_count, TILE), f32),
            pltpu.VMEM((slots, SLAB, TILE), f32),
            pltpu.VMEM((slots, TILE), f32),
            pltpu.VMEM((slots, TILE), f32),
            pltpu.VMEM((ITERS, wide_size, piece, TILE), f32),
            pltpu.VMEM((ITERS, wide_size, piece, TILE), f32),
            dma((CHUNKS + 5,)),
            dma((2,)),
            dma((2 * reach, len(spans))),
            dma((max(1, narrow_size - 1 - reach), len(spans))),
            dma((narrow_size, len(spans))),
            dma((ITERS, PARTS)),
            dma((ITERS, PARTS)),
            dma((ITERS,)),
            dma((ITERS,)),
            dma((ITERS,)),
            dma((ITERS,)),
        ],
        compiler_params=pltpu.CompilerParams(
            collective_id=0, has_side_effects=True, vmem_limit_bytes=67043328
        ),
    )(
        block_cols.T,
        block_counts.T,
        source_features,
        target_features,
        source_mass.reshape(row_count, TILE),
        target_mass.reshape(col_count, TILE),
    )
    rows, cols = pl.pallas_call(
        hand_over,
        out_shape=(
            jax.ShapeDtypeStruct((row_count, TILE), f32),
            jax.ShapeDtypeStruct((col_count, TILE), f32),
        ),
        in_specs=[vmem, vmem],
        out_specs=(vmem, vmem),
    )(rows, cols)
    return rows.reshape(-1), cols.reshape(-1)


def solution(mesh):
    in_specs = (
        P(None, ("wide", "narrow")),
        P(None, "narrow"),
        P("wide"),
        P("narrow"),
        P("wide", "narrow"),
        P("wide", "narrow"),
    )
    out_specs = (P("wide"), P("narrow"))
    return jax.shard_map(
        functools.partial(local, mesh.shape["wide"], mesh.shape["narrow"]),
        mesh=mesh,
        in_specs=in_specs,
        out_specs=out_specs,
        check_vma=False,
    )
```
